32 devices in a mesh: dp: 4 (over z), expert: 4 (over y, x), seq: 2 (over core).
Axes of the slice: x: 2, y: 2, z: 4, core: 2. Of those that a mesh axis runs over, the one named last changes fastest.
Arguments:
- tokens: bfloat16 [2, 16, 2, 640, 768], P(None, ('dp', 'expert'), 'seq'), may hold values from -6 to 6
- previous_gate: float32 [2, 16, 2, 640, 12], P(None, ('dp', 'expert'), 'seq'), may hold values from -3 to 3
- routes: int32 [2, 16, 2, 640, 2], P(None, ('dp', 'expert'), 'seq'), may hold values from 0 to 11, all different within a row; in each aligned block of 640 rows (0 to 639, 640 to 1279, ..., all dimensions but the last counted through in order) at most 160 rows name the same one
- prompt_choice: int32 [2, 16, 2, 1], P(None, ('dp', 'expert'), 'seq'), may hold values from 0 to 3, as said below
- attention_gain: bfloat16 [768], P('dp'), may hold values from 0.5 to 1.5
- query_weight: bfloat16 [768, 768], P('dp'), may hold values from -0.21875 to 0.21875
- key_weight: bfloat16 [768, 768], P('dp'), may hold values from -0.3125 to 0.3125
- value_weight: bfloat16 [768, 768], P('dp'), may hold values from -0.21875 to 0.21875
- output_weight: bfloat16 [768, 768], P('dp'), may hold values from -3 to 3
- feedforward_gain: bfloat16 [768], P('dp'), may hold values from 0.5 to 1.5
- router_weight: bfloat16 [768, 12], P('dp'), may hold values from -0.15625 to 0.15625
- constant_weight: bfloat16 [768, 4], P('dp'), may hold values from -0.21875 to 0.21875
- constant_vector: bfloat16 [2, 768], P(None, 'dp'), may hold values from -5 to 5
- expert_gate: bfloat16 [8, 768, 2048], P('expert', 'dp'), may hold values from -0.21875 to 0.21875
- expert_up: bfloat16 [8, 768, 2048], P('expert', 'dp'), may hold values from -0.21875 to 0.21875
- expert_down: bfloat16 [8, 2048, 768], P('expert', 'dp'), may hold values from -0.25 to 0.25
- cotangent: bfloat16 [2, 16, 2, 640, 768], P(None, ('dp', 'expert'), 'seq'), may hold values from -6 to 6
Outputs:
- mixed: bfloat16 [2, 16, 2, 640, 768], P(None, ('dp', 'expert'), 'seq')
- input_grad: float32 [2, 16, 2, 640, 768], P(None, ('dp', 'expert'), 'seq')
- attention_gain_grad: float32 [768], P('dp')
- query_weight_grad: float32 [768, 768], P('dp')
- key_weight_grad: float32 [768, 768], P('dp')
- value_weight_grad: float32 [768, 768], P('dp')
- output_weight_grad: float32 [768, 768], P('dp')
- feedforward_gain_grad: float32 [768], P('dp')
- router_weight_grad: float32 [768, 12], P('dp')
- constant_weight_grad: float32 [768, 4], P('dp')
- constant_vector_grad: float32 [2, 768], P(None, 'dp')
- expert_gate_grad: float32 [8, 768, 2048], P('expert', 'dp')
- expert_up_grad: float32 [8, 768, 2048], P('expert', 'dp')
- expert_down_grad: float32 [8, 2048, 768], P('expert', 'dp')
The draws below stay inside these ranges and needn't reach their ends.
Inputs may be any that keep to these rules, and one draw needn't show every extreme that they name: `routes`: in each aligned block of 640 rows (one block of one micro-batch) no number is named by more than 160 rows, a bound that some block reaches; a row names two different numbers. `prompt_choice`: in every micro-batch and data group, each of the 4 prompts is chosen by exactly 2 continuations.
All inputs are finite; a program needn't handle non-finite values.
Results may differ from the reference program's by a relative error of at most 0.03.
Values may be sent and summed in bfloat16 or wider, within the bound.
No kernel may reach another device: no remote copies, remote signals or barrier semaphores. Data moves between devices by JAX's collectives and lax.ppermute only.
A program may use at most 272 MiB of HBM per device.

```python
import math
from functools import partial
import jax
import jax.numpy as jnp
import numpy as np
from jax import lax

D = 768
HEADS = 12
HEAD_DIM = 64
FF = 2048
EXPERTS = 8
ROUTES = 12
MB = 2
PROMPT = 1024
CONT_LEN = 128
CONT_DEV = 1
PROMPT_DEV = 512
TOK_DEV = 640
CAP = 160
GROUPS = 16
N_DP = 4
N_EXPERT = 4
N_SEQ = 2


def draw_prompt_choice(key, part):
    per_prompt = N_SEQ * CONT_DEV
    count = N_EXPERT * per_prompt
    balanced = jnp.arange(count, dtype=jnp.int32) // per_prompt
    subkeys = jax.random.split(jax.random.fold_in(key, 17), MB * N_DP)

    def shuffle(subkey):
        return jax.random.permutation(subkey, balanced)
    shuffled = jax.vmap(shuffle)(subkeys)
    return shuffled.reshape(MB, GROUPS, N_SEQ, CONT_DEV).astype(jnp.int32)


def level_of(rng, shape, pieces, least, high):
    def one(dim, blocks):
        heights = jax.random.uniform(jax.random.fold_in(jax.random.fold_in(rng, 6), dim), (blocks,), jnp.float32, least / len(pieces), high / len(pieces))
        return jnp.repeat(jnp.exp(heights), shape[dim] // blocks).reshape((-1,) + (1,) * (len(shape) - dim - 1))

    loudness = one(*pieces[0])
    for cut in pieces[1:]:
        loudness = loudness * one(*cut)
    return loudness


def shared_out(own_key, own, number, rows, amount, top, limit, slope):
    sequence = jax.random.permutation(own_key, amount)
    crowded, ordinary = load_shares(amount, rows * top, limit, slope, True), load_shares(amount, rows * top, limit, slope, False)
    places = jnp.arange(amount)

    def named(sizes, turn):
        used = int((sizes > 0).sum())
        fixed = max(1, used // 4)
        moved = fixed + (places - fixed + turn * (used - fixed)) % max(1, amount - fixed)
        return jnp.zeros((amount,), jnp.int32).at[sequence[jnp.where(places < fixed, places, moved)]].set(jnp.asarray(sizes, jnp.int32))

    sizes = jnp.where(number % 4 == 0, named(crowded, number // 4), named(ordinary, number - number // 4 - 1))
    mixed = jax.random.permutation(jax.random.fold_in(own, 3), amount)
    giver, sink = mixed[0:amount // 2 * 2:2], mixed[1:amount // 2 * 2:2]
    margin = jnp.minimum(sizes[giver] - 1, limit - sizes[sink]) // 2
    margin = jnp.where((giver == sequence[0]) | (sink == sequence[0]) | (sizes[sink] == 0), 0, jnp.maximum(margin, 0))
    moved = jax.random.randint(jax.random.fold_in(own, 4), (amount // 2,), 0, 1 << 20) % (margin + 1)
    sizes = sizes.at[giver].add(-moved).at[sink].add(moved)
    labels = jnp.searchsorted(jnp.cumsum(sizes), jnp.arange(rows * top), side="right").astype(jnp.int32)
    listing = labels.reshape(top, rows).T
    listing = listing[jax.random.permutation(jax.random.fold_in(own, 1), rows)]
    turn = jax.random.randint(jax.random.fold_in(own, 2), (rows, 1), 0, top)
    return jnp.take_along_axis(listing, (jnp.arange(top)[None, :] + turn) % top, axis=1)


def load_shares(count, total, reach, lean, full):
    portions = [(1 << 20) // math.isqrt(grade ** lean) + 1 for grade in range(1, count + 1)]
    largest = reach if full else min(reach, max(-(-total // count), total * portions[0] // sum(portions)))
    least = 1 if total - largest >= count - 1 else 0
    counts, surplus = [largest] + [least] * (count - 1), total - largest - least * (count - 1)
    while surplus > 0:
        movable = [i for i in range(1, count) if counts[i] < largest] or [i for i in range(1, count) if counts[i] < reach]
        pool, remaining = sum([portions[i] for i in movable]), surplus
        for i in movable:
            addition = min(reach - counts[i], max(1, remaining * portions[i] // pool), surplus)
            counts[i] = counts[i] + addition
            surplus = surplus - addition
    return np.array(counts)


def gaussian(key, dims, scale, reach, cuts=(), kind=jnp.bfloat16):
    factor_of = level_of(key, dims, cuts, -0.22, 0.18) if cuts else 1.0
    result = jax.random.normal(key, dims, jnp.float32) * scale * factor_of
    return jnp.minimum(jnp.maximum(result, -reach), reach).astype(kind)


def setup_inputs(seed: int = 0) -> dict:
    key_list = jax.random.split(jax.random.key(seed), 18)
    tokens = gaussian(key_list[0], (MB, GROUPS, N_SEQ, TOK_DEV, D), 1.0, 6.0, ((1, 16), (2, 2)))
    previous_gate = gaussian(key_list[1], (MB, GROUPS, N_SEQ, TOK_DEV, ROUTES), 0.5, 3.0, ((1, 16), (2, 2)), jnp.float32)
    routes_keys = jax.random.split(jax.random.fold_in(key_list[2], 1), MB * GROUPS * N_SEQ * TOK_DEV // TOK_DEV)
    routes_turns = jax.random.permutation(jax.random.fold_in(key_list[2], 3), MB * GROUPS * N_SEQ * TOK_DEV // TOK_DEV)
    routes = jax.vmap(lambda own, number: shared_out(jax.random.fold_in(key_list[2], 2), own, number, TOK_DEV, ROUTES, 2, CAP, 2))(routes_keys, routes_turns).reshape((MB, GROUPS, N_SEQ, TOK_DEV, 2))
    prompt_choice = draw_prompt_choice(jax.random.fold_in(key_list[17], 71), 0)
    attention_gain = jnp.clip(1.0 + 0.1 * jax.random.normal(key_list[4], (D,), jnp.float32), 0.5, 1.5).astype(jnp.bfloat16)
    query_weight = gaussian(key_list[5], (D, D), D ** -0.5, 0.21875, ((0, 4),))
    key_weight = gaussian(key_list[6], (D, D), (D // 2) ** -0.5, 0.3125, ((0, 4),))
    value_weight = gaussian(key_list[7], (D, D), D ** -0.5, 0.21875, ((0, 4),))
    output_weight = gaussian(key_list[8], (D, D), 4 ** -0.5, 3.0, ((0, 4),))
    feedforward_gain = jnp.clip(1.0 + 0.1 * jax.random.normal(key_list[9], (D,), jnp.float32), 0.5, 1.5).astype(jnp.bfloat16)
    router_weight = gaussian(key_list[10], (D, ROUTES), (2 * D) ** -0.5, 0.15625, ((0, 4),))
    constant_weight = gaussian(key_list[11], (D, 4), D ** -0.5, 0.21875, ((0, 4),))
    constant_vector = gaussian(key_list[12], (2, D), 1.0, 5.0, ((1, 4),))
    expert_gate = gaussian(key_list[13], (EXPERTS, D, FF), D ** -0.5, 0.21875, ((0, 4), (1, 4)))
    expert_up = gaussian(key_list[14], (EXPERTS, D, FF), D ** -0.5, 0.21875, ((0, 4), (1, 4)))
    expert_down = gaussian(key_list[15], (EXPERTS, FF, D), (FF // 4) ** -0.5, 0.25, ((0, 4), (1, 4)))
    cotangent = gaussian(key_list[16], (MB, GROUPS, N_SEQ, TOK_DEV, D), 1.0, 6.0, ((1, 16), (2, 2)))
    return {"tokens": tokens, "previous_gate": previous_gate, "routes": routes, "prompt_choice": prompt_choice, "attention_gain": attention_gain, "query_weight": query_weight, "key_weight": key_weight, "value_weight": value_weight, "output_weight": output_weight, "feedforward_gain": feedforward_gain, "router_weight": router_weight, "constant_weight": constant_weight, "constant_vector": constant_vector, "expert_gate": expert_gate, "expert_up": expert_up, "expert_down": expert_down, "cotangent": cotangent}


@jax.custom_vjp
def low(v):
    return lax.optimization_barrier(v.astype(jnp.bfloat16)).astype(jnp.float32)

@jax.custom_vjp
def low_back(v):
    return v

def low_keep(v):
    return (low(v), None)

def low_pass(kept, grad):
    return (grad,)

def back_keep(v):
    return (v, None)

def back_low(kept, grad):
    return (low(grad),)
low.defvjp(low_keep, low_pass)
low_back.defvjp(back_keep, back_low)
precise = lax.Precision.HIGHEST
epsilon = 1e-06
negative = -1e+30
scale_factor = 0.125

def matmul(left, right):
    return jnp.dot(left, right, precision=precise, preferred_element_type=jnp.float32)

def rotate_half(tensor):
    middle = tensor.shape[-1] // 2
    return jnp.concatenate([-tensor[..., middle:], tensor[..., :middle]], axis=-1)

def split_heads(tensor):
    return tensor.reshape(tensor.shape[:-1] + (HEADS, HEAD_DIM))

def rotary(tensor, position):
    middle = HEAD_DIM // 2
    inverse = 10000.0 ** (-jnp.arange(middle, dtype=jnp.float32) * 2.0 / HEAD_DIM)
    angles = position[..., None] * inverse
    cosine_table = jnp.concatenate([jnp.cos(angles), jnp.cos(angles)], axis=-1)[..., None, :]
    sine_table = jnp.concatenate([jnp.sin(angles), jnp.sin(angles)], axis=-1)[..., None, :]
    shaped = split_heads(tensor)
    turned = shaped * cosine_table + rotate_half(shaped) * sine_table
    return turned.reshape(tensor.shape)

def rmsnorm(tensor, gain):
    return tensor * lax.rsqrt(lax.optimization_barrier(jnp.mean(tensor * tensor, axis=-1, keepdims=True)) + epsilon) * gain

def attention(queries, key_rows, value_rows, visible):
    scores = low_back(jnp.einsum('qhd,khd->hqk', queries, key_rows, precision=precise) * scale_factor)
    scores = jnp.where(visible[None], scores, negative)
    probabilities = low(jax.nn.softmax(scores, axis=-1))
    return jnp.einsum('hqk,khd->qhd', probabilities, value_rows, precision=precise)

def group_attention(dense_set, group_tokens, group_choice):
    gain_attn, weight_query, weight_key, weight_value, weight_out = dense_set
    attn_in = low(rmsnorm(group_tokens, gain_attn))
    row_ids = jnp.arange(TOK_DEV, dtype=jnp.int32)
    seq_ids = jnp.arange(N_SEQ, dtype=jnp.int32)
    position = jnp.where(row_ids[None, :] < PROMPT_DEV, seq_ids[:, None] * PROMPT_DEV + row_ids[None, :], PROMPT + (row_ids[None, :] - PROMPT_DEV) % CONT_LEN).astype(jnp.float32)
    queries = low(rotary(low_back(matmul(attn_in, weight_query)), position))
    key_rows = low(rotary(low_back(matmul(attn_in, weight_key)), position))
    value_rows = low(low_back(matmul(attn_in, weight_value)))
    prompt_q = split_heads(queries[:, :, :PROMPT_DEV]).reshape(N_EXPERT, PROMPT, HEADS, HEAD_DIM)
    prompt_k = split_heads(key_rows[:, :, :PROMPT_DEV]).reshape(N_EXPERT, PROMPT, HEADS, HEAD_DIM)
    prompt_v = split_heads(value_rows[:, :, :PROMPT_DEV]).reshape(N_EXPERT, PROMPT, HEADS, HEAD_DIM)
    prompt_ids = jnp.arange(PROMPT, dtype=jnp.int32)
    causal = prompt_ids[None, :] <= prompt_ids[:, None]
    prompt_out = jax.vmap(attention, in_axes=(0, 0, 0, None))(prompt_q, prompt_k, prompt_v, causal)
    count = N_EXPERT * N_SEQ * CONT_DEV
    picks = group_choice.reshape(count)
    cont_q = split_heads(queries[:, :, PROMPT_DEV:]).reshape(count, CONT_LEN, HEADS, HEAD_DIM)
    cont_k = jnp.concatenate([jnp.take(prompt_k, picks, axis=0), split_heads(key_rows[:, :, PROMPT_DEV:]).reshape(count, CONT_LEN, HEADS, HEAD_DIM)], axis=1)
    cont_v = jnp.concatenate([jnp.take(prompt_v, picks, axis=0), split_heads(value_rows[:, :, PROMPT_DEV:]).reshape(count, CONT_LEN, HEADS, HEAD_DIM)], axis=1)
    cont_rows = jnp.arange(CONT_LEN, dtype=jnp.int32)
    key_cols = jnp.arange(PROMPT + CONT_LEN, dtype=jnp.int32)
    cont_visible = (key_cols[None, :] < PROMPT) | (key_cols[None, :] - PROMPT <= cont_rows[:, None])
    cont_out = jax.vmap(attention, in_axes=(0, 0, 0, None))(cont_q, cont_k, cont_v, cont_visible)
    attn_out = jnp.concatenate([prompt_out.reshape(N_EXPERT, N_SEQ, PROMPT_DEV, D), cont_out.reshape(N_EXPERT, N_SEQ, CONT_DEV * CONT_LEN, D)], axis=2)
    attn_low = low(low_back(attn_out))
    return group_tokens + low_back(matmul(attn_low, weight_out))

def expert_pass(parts):
    rows_in, weight_gate, weight_up, weight_down = parts
    gate_pre = low_back(matmul(rows_in, weight_gate))
    up_pre = low_back(matmul(rows_in, weight_up))
    hidden = low(jax.nn.silu(gate_pre) * up_pre)
    return low(low_back(matmul(hidden, weight_down)))

def mixture(moe_set, hidden_state, gate_prev, route_rows):
    gain_ffn, weight_router, weight_const, vector_const, weight_gate, weight_up, weight_down = moe_set
    blocks = hidden_state.shape[0]
    normed = rmsnorm(hidden_state, gain_ffn)
    normed_low = low(normed)
    logits = matmul(normed_low, weight_router) + gate_prev
    route_marks = (route_rows[..., None] == jnp.arange(ROUTES, dtype=jnp.int32)).astype(jnp.float32)
    chosen = lax.optimization_barrier(jnp.sum(logits[:, :, None, :] * route_marks, axis=-1))
    gate_weights = jax.nn.softmax(chosen, axis=-1)
    flattened = route_rows.reshape(blocks, TOK_DEV * 2)
    one_hot = (flattened[..., None] == jnp.arange(ROUTES, dtype=jnp.int32)).astype(jnp.int32)
    before = jnp.cumsum(one_hot, axis=1, dtype=jnp.int32) - one_hot
    slot_rows = lax.optimization_barrier(jnp.sum(before * one_hot, axis=-1)).reshape(blocks, TOK_DEV, 2)
    ffn_mask = (route_rows < EXPERTS).astype(jnp.float32)
    expert_ids = jnp.minimum(route_rows, EXPERTS - 1)
    block_ids = jnp.broadcast_to(jnp.arange(blocks, dtype=jnp.int32)[:, None], (blocks, TOK_DEV))
    buffer = jnp.zeros((blocks, EXPERTS, CAP, D), jnp.float32)
    for slot_number in range(2):
        update = low_back(normed_low) * ffn_mask[..., slot_number, None]
        buffer = buffer.at[block_ids, expert_ids[..., slot_number], slot_rows[..., slot_number]].add(update)
    by_expert = buffer.transpose(1, 0, 2, 3).reshape(EXPERTS, blocks * CAP, D)
    results = lax.map(jax.checkpoint(expert_pass), (by_expert, weight_gate, weight_up, weight_down))
    results = results.reshape(EXPERTS, blocks, CAP, D).transpose(1, 0, 2, 3)
    alphas = jax.nn.softmax(matmul(normed_low, weight_const).reshape(blocks, TOK_DEV, 2, 2), axis=-1)
    const_out = alphas[..., 0:1] * normed[:, :, None, :] + alphas[..., 1:2] * vector_const
    mixed_rows = hidden_state
    for slot_number in range(2):
        route_now = route_rows[..., slot_number]
        ffn_part = results[block_ids, expert_ids[..., slot_number], slot_rows[..., slot_number]] * ffn_mask[..., slot_number, None]
        copy_part = (route_now == EXPERTS + 1).astype(jnp.float32)[..., None] * normed
        const_part = (route_now == EXPERTS + 2).astype(jnp.float32)[..., None] * const_out[:, :, 0] + (route_now == EXPERTS + 3).astype(jnp.float32)[..., None] * const_out[:, :, 1]
        mixed_rows = mixed_rows + gate_weights[..., slot_number:slot_number + 1] * (ffn_part + copy_part + const_part)
    return mixed_rows

def forward_micro(weights, token_rows, gate_prev, route_rows, choice_rows):
    gain_attn, weight_query, weight_key, weight_value, weight_out, gain_ffn, weight_router, weight_const, vector_const, weight_gate, weight_up, weight_down = weights
    grouped = token_rows.reshape(N_DP, N_EXPERT, N_SEQ, TOK_DEV, D)
    choices_grouped = choice_rows.reshape(N_DP, N_EXPERT, N_SEQ, CONT_DEV)
    attend = jax.checkpoint(partial(group_attention, (gain_attn, weight_query, weight_key, weight_value, weight_out)))

    def attend_pair(pair):
        return attend(pair[0], pair[1])
    states = lax.map(attend_pair, (grouped, choices_grouped))
    hidden_state = states.reshape(GROUPS * N_SEQ, TOK_DEV, D)
    mixed_rows = mixture((gain_ffn, weight_router, weight_const, vector_const, weight_gate, weight_up, weight_down), hidden_state, gate_prev.reshape(GROUPS * N_SEQ, TOK_DEV, ROUTES), route_rows.reshape(GROUPS * N_SEQ, TOK_DEV, 2))
    return mixed_rows.reshape(GROUPS, N_SEQ, TOK_DEV, D)

def reference(tokens, previous_gate, routes, prompt_choice, attention_gain, query_weight, key_weight, value_weight, output_weight, feedforward_gain, router_weight, constant_weight, constant_vector, expert_gate, expert_up, expert_down, cotangent):
    weights = tuple((entry.astype(jnp.float32) for entry in (attention_gain, query_weight, key_weight, value_weight, output_weight, feedforward_gain, router_weight, constant_weight, constant_vector, expert_gate, expert_up, expert_down)))
    mixed_parts = []
    input_parts = []
    totals = None
    for micro_index in range(MB):

        def forward_one(weight_set, token_rows):
            return forward_micro(weight_set, token_rows, previous_gate[micro_index], routes[micro_index], prompt_choice[micro_index])
        output, pullback = jax.vjp(forward_one, weights, tokens[micro_index].astype(jnp.float32))
        weight_grads, input_grad = pullback(cotangent[micro_index].astype(jnp.float32))
        mixed_parts.append(output.astype(jnp.bfloat16))
        input_parts.append(input_grad)
        totals = weight_grads if totals is None else jax.tree.map(jnp.add, totals, weight_grads)
    return (jnp.stack(mixed_parts), jnp.stack(input_parts), totals[0], totals[1], totals[2], totals[3], totals[4], totals[5], totals[6], totals[7], totals[8], totals[9], totals[10], totals[11])
```

```python
import jax
import jax.numpy as jnp
from jax import lax
from jax.experimental import pallas as pl
from jax.experimental.pallas import tpu as pltpu
from jax.sharding import PartitionSpec as P

HEADS = 12
HEAD_DIM = 64
PROMPT = 1024
CONT_LEN = 128

precise = lax.Precision.HIGHEST
epsilon = 1e-06
negative = -1e30
scale_factor = 0.125
f32 = jnp.float32
bf16 = jnp.bfloat16


def dot(a, b):
    return jnp.dot(a, b, preferred_element_type=f32)


def dot_nt(a, b):
    return lax.dot_general(a, b, (((a.ndim - 1,), (b.ndim - 1,)), ((), ())), preferred_element_type=f32)


def dot_tn(a, b):
    return lax.dot_general(a, b, (((0,), (0,)), ((), ())), preferred_element_type=f32)


QB = 256
LANES = 128


def turn(t, cos, sin, sign):
    lane = lax.broadcasted_iota(jnp.int32, t.shape, 1)
    partner = jnp.where(lane % HEAD_DIM < HEAD_DIM // 2, pltpu.roll(t, 96, 1), pltpu.roll(t, 32, 1))
    return t * cos + sign * (partner * sin)


def qkv_kernel(x_ref, gain_ref, w_ref, cos_ref, sin_ref, qkv_ref, in_ref):
    x = x_ref[0].astype(f32)
    inv = lax.rsqrt(jnp.mean(x * x, axis=-1, keepdims=True) + epsilon)
    a = (x * inv * gain_ref[...]).astype(bf16)
    in_ref[0] = a
    cos = cos_ref[...]
    sin = sin_ref[...]
    for c in range(w_ref.shape[1] // LANES):
        cols = slice(c * LANES, (c + 1) * LANES)
        t = dot(a, w_ref[:, cols])
        if c % 3 < 2:
            t = turn(t, cos, sin, 1.0)
        qkv_ref[0, :, cols] = t.astype(bf16)


def qkv_call(x, gain, w, cos, sin):
    m, rows, d = x.shape
    width = w.shape[1] // (3 * LANES) * 3 * LANES
    half = rows // 2
    return pl.pallas_call(
        qkv_kernel,
        grid=(m, 2),
        in_specs=[
            pl.BlockSpec((1, half, d), lambda i, j: (i, j, 0)),
            pl.BlockSpec((1, d), lambda i, j: (0, 0)),
            pl.BlockSpec((d, width), lambda i, j: (0, 0)),
            pl.BlockSpec((half, LANES), lambda i, j: (j, 0)),
            pl.BlockSpec((half, LANES), lambda i, j: (j, 0)),
        ],
        out_specs=[
            pl.BlockSpec((1, half, width), lambda i, j: (i, j, 0)),
            pl.BlockSpec((1, half, d), lambda i, j: (i, j, 0)),
        ],
        out_shape=[jax.ShapeDtypeStruct((m, rows, width), bf16), jax.ShapeDtypeStruct((m, rows, d), bf16)],
        name="qkv",
    )(x, gain, w, cos, sin)


def head_mask(t, h):
    lane = lax.broadcasted_iota(jnp.int32, t.shape, 1)
    return jnp.where(lane // HEAD_DIM == h, t, jnp.zeros_like(t))


def last_block_mask(i, blocks):
    r = lax.broadcasted_iota(jnp.int32, (QB, QB), 0)
    c = lax.broadcasted_iota(jnp.int32, (QB, QB), 1)
    see = r <= c
    if i == blocks:
        see = see & (r // CONT_LEN == c // CONT_LEN)
    return see


def flip(t):
    return t.astype(f32).T.astype(bf16)


def attend_kernel(qkv_ref, o_ref, lse_ref):
    rows = qkv_ref.shape[1]
    blocks = PROMPT // QB
    k = qkv_ref[0, :, LANES : 2 * LANES]
    vt = flip(qkv_ref[0, :, 2 * LANES :])
    for i in range(rows // QB):
        n = (i + 1) * QB
        q = qkv_ref[0, i * QB : n, :LANES].astype(f32) * scale_factor
        see = last_block_mask(i, blocks)
        outs = []
        for h in range(2):
            qm = head_mask(q, h).astype(bf16)
            s_last = jnp.where(see, dot_nt(k[n - QB : n], qm), negative)
            s = s_last if i == 0 else jnp.concatenate([dot_nt(k[: n - QB], qm), s_last], axis=0)
            top = jnp.max(s, axis=0, keepdims=True)
            p = jnp.exp(s - top)
            total = jnp.sum(p, axis=0, keepdims=True)
            ot = dot(vt[h * HEAD_DIM : (h + 1) * HEAD_DIM, :n], p.astype(bf16))
            outs.append(ot / total)
            lse_ref[0, 0, h : h + 1, i * QB : n] = top + jnp.log(total)
        o_ref[0, i * QB : n, :] = jnp.concatenate(outs, axis=0).T.astype(bf16)


def attend_call(qkv):
    m, rows, width = qkv.shape
    pairs = width // (3 * LANES)
    return pl.pallas_call(
        attend_kernel,
        grid=(m, pairs),
        in_specs=[pl.BlockSpec((1, rows, 3 * LANES), lambda i, j: (i, 0, j))],
        out_specs=[
            pl.BlockSpec((1, rows, LANES), lambda i, j: (i, 0, j)),
            pl.BlockSpec((1, 1, 2, rows), lambda i, j: (i, j, 0, 0)),
        ],
        out_shape=[
            jax.ShapeDtypeStruct((m, rows, pairs * LANES), bf16),
            jax.ShapeDtypeStruct((m, pairs, 2, rows), f32),
        ],
        name="attend",
    )(qkv)


def attend_back_kernel(qkv_ref, do_p_ref, do_v_ref, lse_ref, cos_ref, sin_ref, low_ref, dk_ref, dv_ref):
    rows = qkv_ref.shape[1]
    blocks = PROMPT // QB
    k = qkv_ref[0, :, LANES : 2 * LANES]
    v = qkv_ref[0, :, 2 * LANES :]
    kt = flip(k)
    dk_ref[...] = jnp.zeros_like(dk_ref)
    dv_ref[...] = jnp.zeros_like(dv_ref)
    for i in range(rows // QB):
        n = (i + 1) * QB
        own = slice(i * QB, n)
        q = qkv_ref[0, own, :LANES].astype(f32) * scale_factor
        do = (do_p_ref[0, own, :] if i < blocks else do_v_ref[0, (i - blocks) * QB : (i - blocks + 1) * QB, :]).astype(f32)
        see = last_block_mask(i, blocks)
        outs = []
        for h in range(2):
            qm = head_mask(q, h).astype(bf16)
            dom = head_mask(do, h).astype(bf16)
            s_last = jnp.where(see, dot_nt(k[n - QB : n], qm), negative)
            s = s_last if i == 0 else jnp.concatenate([dot_nt(k[: n - QB], qm), s_last], axis=0)
            p = jnp.exp(s - lse_ref[0, 0, h : h + 1, own])
            dp = dot_nt(v[:n], dom)
            ds = (p * (dp - jnp.sum(dp * p, axis=0, keepdims=True))).astype(bf16)
            dv_ref[:n, :] += dot(p.astype(bf16), dom)
            dk_ref[:n, :] += dot(ds, qm)
            outs.append(dot(kt[h * HEAD_DIM : (h + 1) * HEAD_DIM, :n], ds))
        dq = jnp.concatenate(outs, axis=0).T * scale_factor
        low_ref[0, own, :LANES] = turn(dq, cos_ref[own, :], sin_ref[own, :], -1.0).astype(bf16)
    low_ref[0, :, LANES : 2 * LANES] = turn(dk_ref[...], cos_ref[...], sin_ref[...], -1.0).astype(bf16)
    low_ref[0, :, 2 * LANES :] = dv_ref[...].astype(bf16)


def attend_back_call(qkv, do_p, do_v, lse, cos, sin):
    m, rows, width = qkv.shape
    pairs = width // (3 * LANES)
    return pl.pallas_call(
        attend_back_kernel,
        grid=(m, pairs),
        in_specs=[
            pl.BlockSpec((1, rows, 3 * LANES), lambda i, j: (i, 0, j)),
            pl.BlockSpec((1, do_p.shape[1], LANES), lambda i, j: (i, 0, j)),
            pl.BlockSpec((1, do_v.shape[1], LANES), lambda i, j: (i, 0, j)),
            pl.BlockSpec((1, 1, 2, rows), lambda i, j: (i, j, 0, 0)),
            pl.BlockSpec((rows, LANES), lambda i, j: (0, 0)),
            pl.BlockSpec((rows, LANES), lambda i, j: (0, 0)),
        ],
        out_specs=pl.BlockSpec((1, rows, 3 * LANES), lambda i, j: (i, 0, j)),
        out_shape=jax.ShapeDtypeStruct((m, rows, width), bf16),
        scratch_shapes=[pltpu.VMEM((rows, LANES), f32), pltpu.VMEM((rows, LANES), f32)],
        name="attend_back",
    )(qkv, do_p, do_v, lse, cos, sin)


def din_kernel(low_ref, w_ref, x_ref, d_ref, gain_ref):
    @pl.when((pl.program_id(0) == 0) & (pl.program_id(1) == 0))
    def _():
        gain_ref[...] = jnp.zeros_like(gain_ref)

    d = dot_nt(low_ref[0], w_ref[...])
    x = x_ref[0].astype(f32)
    inv = lax.rsqrt(jnp.mean(x * x, axis=-1, keepdims=True) + epsilon)
    gain_ref[...] += jnp.sum(d * (x * inv), axis=0, keepdims=True)
    d_ref[0] = d.astype(bf16)


def din_call(low, w, x):
    m, rows, width = low.shape
    d = x.shape[2]
    half = rows // 2
    return pl.pallas_call(
        din_kernel,
        grid=(m, 2),
        in_specs=[
            pl.BlockSpec((1, half, width), lambda i, j: (i, j, 0)),
            pl.BlockSpec((d, width), lambda i, j: (0, 0)),
            pl.BlockSpec((1, half, d), lambda i, j: (i, j, 0)),
        ],
        out_specs=[
            pl.BlockSpec((1, half, d), lambda i, j: (i, j, 0)),
            pl.BlockSpec((1, d), lambda i, j: (0, 0)),
        ],
        out_shape=[jax.ShapeDtypeStruct((m, rows, d), bf16), jax.ShapeDtypeStruct((1, d), f32)],
        name="din",
    )(low, w, x)


def per_device(
    tokens,
    previous_gate,
    routes,
    prompt_choice,
    attention_gain,
    query_weight,
    key_weight,
    value_weight,
    output_weight,
    feedforward_gain,
    router_weight,
    constant_weight,
    constant_vector,
    expert_gate,
    expert_up,
    expert_down,
    cotangent,
):
    MB, R, D = tokens.shape[0], tokens.shape[3], tokens.shape[4]
    C = prompt_choice.shape[3]
    E = lax.axis_size("expert")
    S = lax.axis_size("seq")
    PH = PROMPT // S
    CR = C * CONT_LEN
    cap = R // 4
    local_experts = expert_gate.shape[0]
    all_experts = local_experts * E
    routes_n = all_experts + 4
    HW = D // S
    e_index = lax.axis_index("expert")
    s_index = lax.axis_index("seq")
    shard = query_weight.shape[0]
    dense_axes = ("dp", "expert")
    all_axes = ("dp", "expert", "seq")
    pair = ("expert", "seq")

    toks = tokens[:, 0, 0]
    cont_toks = lax.all_gather(toks[:, PH:].reshape(MB, C, CONT_LEN, D), pair, axis=0)
    prompt_toks = lax.all_gather(toks[:, :PH], "seq", axis=1, tiled=True)
    choices = lax.all_gather(prompt_choice[:, 0, 0], pair, axis=0)
    choices = choices.transpose(1, 0, 2).reshape(MB, E * S * C)
    chosen_i = (choices[:, :, None] == jnp.arange(E)[None, None, :]).astype(jnp.int32)
    rank = jnp.sum((jnp.cumsum(chosen_i, axis=1) - chosen_i) * chosen_i, axis=2)
    slots = S * C
    n_cont = E * S * C
    here = choices == e_index
    at_slot = here[:, None, :] & (rank[:, None, :] == jnp.arange(slots)[None, :, None])
    visit_id = jnp.sum(jnp.where(at_slot, jnp.arange(n_cont), 0), axis=2)
    visit_row = ((visit_id // C) * MB + jnp.arange(MB)[:, None]) * C + visit_id % C
    my_choice = prompt_choice[:, 0, 0]

    def pick_visitors(t):
        w = t.shape[-1]
        return jnp.take(t.reshape(E * S * MB * C, CONT_LEN, w), visit_row.reshape(-1), axis=0).reshape(MB, slots * CONT_LEN, w)

    def send_home(t):
        w = t.shape[-1]
        t = t.reshape(MB, slots, 1, CONT_LEN, w)
        marks = at_slot.reshape(MB, slots, n_cont, 1, 1)
        zero = jnp.zeros((), t.dtype)
        out = jnp.where(marks[:, 0], t[:, 0], zero)
        for j in range(1, slots):
            out = jnp.where(marks[:, j], t[:, j], out)
        out = out.reshape(MB, E * S, C, CONT_LEN, w).transpose(1, 0, 2, 3, 4)
        return lax.all_to_all(out, pair, split_axis=0, concat_axis=0, tiled=True)

    rows_all = jnp.concatenate([prompt_toks, pick_visitors(cont_toks)], axis=1)

    n16 = shard // E
    half_shard = shard // S

    def mine(w):
        return lax.dynamic_slice(w, (0, s_index * HW), (shard, HW)).reshape(shard, HW // LANES, 1, LANES)

    part_a = jnp.concatenate(
        [
            jnp.concatenate([mine(query_weight), mine(key_weight), mine(value_weight)], axis=2).reshape(shard, 3 * HW),
            jnp.pad(attention_gain[:, None], ((0, 0), (0, LANES - 1))),
        ],
        axis=1,
    )
    n_dp = lax.axis_size("dp")
    full_a = lax.all_to_all(
        jnp.broadcast_to(part_a[None], (n_dp,) + part_a.shape), "dp", split_axis=0, concat_axis=0, tiled=True
    ).reshape(D, 3 * HW + LANES)
    gain_attn = full_a[:, 3 * HW].astype(f32)
    small_cols = routes_n + 4 + 1 + 2
    part_b = jnp.concatenate(
        [
            output_weight,
            router_weight,
            constant_weight,
            feedforward_gain[:, None],
            constant_vector.T,
            jnp.zeros((shard, LANES - small_cols), bf16),
        ],
        axis=1,
    )
    part_b = lax.dynamic_slice(part_b, (s_index * half_shard, 0), (half_shard, D + LANES))
    full_b = lax.all_gather(part_b, ("dp", "seq"), axis=0, tiled=True)
    w_out = full_b[:, :D]
    w_small = full_b[:, D : D + routes_n + 4]
    gain_ffn = full_b[:, D + routes_n + 4].astype(f32)
    vectors = full_b[:, D + routes_n + 5 : D + routes_n + 7].astype(f32).T

    def own_expert(w):
        return lax.dynamic_index_in_dim(w, s_index, 0, keepdims=False)

    w_gate = lax.all_gather(own_expert(expert_gate), "dp", axis=0, tiled=True)
    w_up = lax.all_gather(own_expert(expert_up), "dp", axis=0, tiled=True)
    w_down = lax.all_gather(own_expert(expert_down), "dp", axis=0, tiled=True)

    inverse = 10000.0 ** (-jnp.arange(HEAD_DIM // 2, dtype=f32) * 2.0 / HEAD_DIM)
    pos = jnp.concatenate([jnp.arange(PROMPT), PROMPT + jnp.arange(slots * CONT_LEN) % CONT_LEN])
    angle = pos.astype(f32)[:, None] * inverse
    cos = jnp.concatenate([jnp.cos(angle)] * 4, axis=-1)
    sin = jnp.concatenate([-jnp.sin(angle), jnp.sin(angle)] * 2, axis=-1)
    qkv, attn_in = qkv_call(rows_all, gain_attn[None], full_a, cos, sin)
    heads_out, lse = attend_call(qkv)
    prompt_out = heads_out[:, :PROMPT].reshape(MB, S, PH, HW).transpose(1, 0, 2, 3)
    prompt_out = lax.all_to_all(prompt_out, "seq", split_axis=0, concat_axis=0, tiled=True)
    cont_out = jnp.sum(send_home(heads_out[:, PROMPT:]).reshape(E, S, MB, CR, HW), axis=0)
    attn = jnp.concatenate([prompt_out, cont_out], axis=2)
    attn_low = jnp.concatenate([attn[i] for i in range(S)], axis=-1).reshape(MB * R, D)
    N = MB * R
    x = toks.reshape(N, D).astype(f32)
    h = x + dot(attn_low, w_out)
    inv2 = lax.rsqrt(jnp.mean(h * h, axis=-1, keepdims=True) + epsilon)
    hhat = h * inv2
    normed = hhat * gain_ffn
    normed_low = normed.astype(bf16)
    dy_low = cotangent[:, 0, 0].reshape(N, D)
    dy = dy_low.astype(f32)

    route = routes[:, 0, 0].reshape(N, 2)
    marks = (route[:, :, None] == jnp.arange(routes_n)).astype(f32)
    small = dot(normed_low, w_small)
    logits = small[:, :routes_n] + previous_gate[:, 0, 0].reshape(N, routes_n)
    chosen_logits = jnp.sum(logits[:, None, :] * marks, axis=-1)
    gate = jax.nn.softmax(chosen_logits, axis=-1)
    alphas = jax.nn.softmax(small[:, routes_n:].reshape(N, 2, 2), axis=-1)
    lower = (jnp.arange(R)[None, :] < jnp.arange(R)[:, None]).astype(bf16)
    marks_low = marks.astype(bf16).reshape(MB, R, 2 * routes_n)
    before = jnp.einsum("rs,msk->mrk", lower, marks_low, preferred_element_type=f32).reshape(MB, R, 2, routes_n)
    first_count = jnp.sum(marks.reshape(MB, R, 2, routes_n)[:, :, 0], axis=1)
    before = before + jnp.stack([jnp.zeros_like(first_count), first_count], axis=1)[:, None]
    ranks = jnp.sum(before.reshape(N, 2, routes_n) * marks, axis=-1).astype(jnp.int32)
    is_ffn = route < all_experts
    index = jnp.where(is_ffn, route * cap + ranks, -1).reshape(MB, R, 2)
    n_slots = all_experts * cap
    onehot = [(index[:, :, i, None] == jnp.arange(n_slots)).astype(bf16) for i in range(2)]
    both = onehot[0] + onehot[1]
    sent_rows = jnp.einsum("mrs,mrd->msd", both, normed_low.reshape(MB, R, D), preferred_element_type=f32).astype(bf16)
    sent_dy = jnp.einsum("mrs,mrd->msd", both, dy_low.reshape(MB, R, D), preferred_element_type=f32)
    gate_m = gate.reshape(MB, R, 2)
    slot_gate = jnp.sum(
        jnp.where(onehot[0] > 0, gate_m[:, :, 0:1], 0.0) + jnp.where(onehot[1] > 0, gate_m[:, :, 1:2], 0.0), axis=1
    )
    sent_dy = (sent_dy * slot_gate[:, :, None]).astype(bf16)

    def to_experts(t):
        return lax.all_to_all(t.reshape(all_experts, cap, D), pair, split_axis=0, concat_axis=0, tiled=True)

    results = []
    back = []
    sums = None
    for m in range(MB):
        rows = to_experts(sent_rows[m]).reshape(-1, D)
        grads = to_experts(sent_dy[m]).reshape(-1, D)
        gate_pre = dot(rows, w_gate)
        up_pre = dot(rows, w_up)
        sig = jax.nn.sigmoid(gate_pre)
        act = gate_pre * sig
        hidden = (act * up_pre).astype(bf16)
        out = dot(hidden, w_down).astype(bf16)
        dhid = dot_nt(grads, w_down)
        d_up = (dhid * act).astype(bf16)
        d_gate = (dhid * up_pre * sig * (1.0 + gate_pre * (1.0 - sig))).astype(bf16)
        d_rows = (dot_nt(d_gate, w_gate) + dot_nt(d_up, w_up)).astype(bf16)
        parts = (dot_tn(rows, d_gate), dot_tn(rows, d_up), dot_tn(hidden, grads))
        sums = parts if sums is None else tuple(a + b for a, b in zip(sums, parts))
        results.append(to_experts(out).reshape(n_slots, D))
        back.append(to_experts(d_rows).reshape(n_slots, D))

    def scatter_dp(g):
        return lax.psum_scatter(g.astype(bf16), "dp", scatter_dimension=0, tiled=True)

    expert_parts = [scatter_dp(g) for g in sums]
    expert_outs = [lax.all_gather(g, "seq", axis=0).astype(f32) for g in expert_parts]

    ffn = [
        jnp.stack([dot(onehot[i][m], results[m]) for m in range(MB)]).reshape(N, D) for i in range(2)
    ]
    d_ffn = jnp.stack([dot(both[m], back[m]) for m in range(MB)]).reshape(N, D)
    const = [alphas[:, c, 0:1] * normed + alphas[:, c, 1:2] * vectors[c] for c in range(2)]
    mark_of = lambda i, r: marks[:, i, r : r + 1]
    branch = [
        ffn[i]
        + mark_of(i, all_experts + 1) * normed
        + mark_of(i, all_experts + 2) * const[0]
        + mark_of(i, all_experts + 3) * const[1]
        for i in range(2)
    ]
    mixed = h + gate[:, 0:1] * branch[0] + gate[:, 1:2] * branch[1]
    d_gates = jnp.stack([jnp.sum(dy * b, axis=-1) for b in branch], axis=-1)
    d_chosen = gate * (d_gates - jnp.sum(gate * d_gates, axis=-1, keepdims=True))
    d_logits = jnp.sum(d_chosen[:, :, None] * marks, axis=1)
    weight_of = lambda r: jnp.sum(gate * marks[:, :, r], axis=-1, keepdims=True)
    dn = d_ffn + weight_of(all_experts + 1) * dy
    dz = []
    d_vec = []
    dyn = jnp.sum(dy * normed, axis=-1, keepdims=True)
    for c in range(2):
        wt = weight_of(all_experts + 2 + c)
        dn = dn + alphas[:, c, 0:1] * wt * dy
        d_alpha = jnp.concatenate([wt * dyn, wt * jnp.sum(dy * vectors[c], axis=-1, keepdims=True)], axis=-1)
        dz.append(alphas[:, c] * (d_alpha - jnp.sum(alphas[:, c] * d_alpha, axis=-1, keepdims=True)))
        d_vec.append(jnp.sum(alphas[:, c, 1:2] * wt * dy, axis=0))
    d_small = jnp.concatenate([d_logits] + dz, axis=1)
    g_small = jnp.dot(normed_low.astype(f32).T, d_small, precision=precise)
    dn = dn + jnp.dot(d_small, w_small.astype(f32).T, precision=precise)
    g_gain_ffn = jnp.sum(dn * hhat, axis=0)
    u = dn * gain_ffn
    dh = dy + inv2 * (u - hhat * jnp.mean(u * hhat, axis=-1, keepdims=True))
    dh_low = dh.astype(bf16)
    g_out = dot_tn(attn_low, dh_low)
    cols = jnp.concatenate(
        [g_out, g_small, g_gain_ffn[:, None], d_vec[0][:, None], d_vec[1][:, None], jnp.zeros((D, LANES - routes_n - 7), f32)],
        axis=1,
    ).astype(bf16)

    def sum_shards(t, axes, count):
        t = lax.all_to_all(t.reshape(count, t.shape[0] // count, t.shape[1]), axes, split_axis=0, concat_axis=0, tiled=True)
        return jnp.sum(t.astype(f32), axis=0).astype(bf16)

    red_b = sum_shards(cols, all_axes, n_dp * E * S)
    red_b = lax.all_gather(red_b, pair, axis=0, tiled=True).astype(f32)
    d_attn = jnp.stack([dot_nt(dh_low, w_out[i * HW : (i + 1) * HW]) for i in range(S)]).astype(bf16)
    d_attn = d_attn.reshape(S, MB, R, HW)
    d_cont = d_attn[:, :, PH:].reshape(1, S, MB, C, CONT_LEN, HW)
    goes = my_choice[None] == jnp.arange(E)[:, None, None]
    d_cont = jnp.where(goes[:, None, :, :, None, None], d_cont, jnp.zeros((), bf16)).reshape(E * S, MB, C, CONT_LEN, HW)
    d_vis = pick_visitors(lax.all_to_all(d_cont, pair, split_axis=0, concat_axis=0, tiled=True))
    d_prompt = lax.all_to_all(d_attn[:, :, :PH], "seq", split_axis=0, concat_axis=0, tiled=True)
    d_prompt = d_prompt.transpose(1, 0, 2, 3).reshape(MB, PROMPT, HW)
    low = attend_back_call(qkv, d_prompt, d_vis, lse, cos, sin)
    d_in, gain_part = din_call(low, full_a, rows_all)
    g_qkv = dot_tn(attn_in.reshape(-1, D), low.reshape(-1, 3 * HW))
    red_a = jnp.concatenate([g_qkv, jnp.pad(gain_part.T, ((0, 0), (0, LANES - 1)))], axis=1).astype(bf16)
    red_a = sum_shards(red_a, dense_axes, n_dp * E)
    red_a = lax.all_gather(red_a, pair, axis=0).astype(f32)
    g_gain_attn = jnp.sum(red_a[:, :, 3 * HW].reshape(E, S, n16), axis=1).reshape(shard)
    red_a = red_a[:, :, : 3 * HW].reshape(E, S, n16, HW // LANES, 3, LANES)
    red_a = red_a.transpose(4, 0, 2, 1, 3, 5).reshape(3, shard, D)
    d_cont = jnp.sum(send_home(d_in[:, PROMPT:]).astype(f32), axis=0).reshape(MB, CR, D)
    d_halves = d_in[:, :PROMPT].reshape(MB, S, PH, D)
    own = lax.dynamic_index_in_dim(d_halves, s_index, 1, keepdims=False)
    other = lax.dynamic_index_in_dim(d_halves, 1 - s_index, 1, keepdims=False)
    swap = [(i, (i + 1) % S) for i in range(S)]
    d_own = own.astype(f32) + lax.ppermute(other, "seq", swap).astype(f32)
    d_in = jnp.concatenate([d_own, d_cont], axis=1).reshape(N, D)
    inv1 = lax.rsqrt(jnp.mean(x * x, axis=-1, keepdims=True) + epsilon)
    xhat = x * inv1
    u1 = d_in * gain_attn
    d_input = dh + inv1 * (u1 - xhat * jnp.mean(u1 * xhat, axis=-1, keepdims=True))

    o = D + routes_n
    return (
        mixed.astype(bf16).reshape(MB, 1, 1, R, D),
        d_input.reshape(MB, 1, 1, R, D),
        g_gain_attn,
        red_a[0],
        red_a[1],
        red_a[2],
        red_b[:, :D],
        red_b[:, o + 4],
        red_b[:, D:o],
        red_b[:, o : o + 4],
        red_b[:, o + 5 : o + 7].T,
        expert_outs[0],
        expert_outs[1],
        expert_outs[2],
    )


def solution(mesh):
    rows = P(None, ("dp", "expert"), "seq", None, None)
    in_specs = (
        rows,
        rows,
        rows,
        P(None, ("dp", "expert"), "seq", None),
        P("dp"),
        P("dp", None),
        P("dp", None),
        P("dp", None),
        P("dp", None),
        P("dp"),
        P("dp", None),
        P("dp", None),
        P(None, "dp"),
        P("expert", "dp", None),
        P("expert", "dp", None),
        P("expert", "dp", None),
        rows,
    )
    out_specs = (
        rows,
        rows,
        P("dp"),
        P("dp", None),
        P("dp", None),
        P("dp", None),
        P("dp", None),
        P("dp"),
        P("dp", None),
        P("dp", None),
        P(None, "dp"),
        P("expert", "dp", None),
        P("expert", "dp", None),
        P("expert", "dp", None),
    )
    return jax.shard_map(per_device, mesh=mesh, in_specs=in_specs, out_specs=out_specs, check_vma=False)
```
